32 devices in a mesh: rep: 4 (over y, core), grp: 4 (over z), ctx: 2 (over x).
Axes of the slice: x: 2, y: 2, z: 4, core: 2. Of those that a mesh axis runs over, the one named last changes fastest.
Arguments:
- hidden: bfloat16 [16, 512, 2048], P(('rep', 'grp'), 'ctx'), may hold values from -6 to 6
- positions: int32 [16, 512], P(('rep', 'grp')), may hold values from 0 to 511, as said below
- cotangent: bfloat16 [16, 512, 2048], P(('rep', 'grp'), 'ctx'), may hold values from -6 to 6
- attention_params: float32 [3072, 2048], P(('grp', 'ctx')), may hold values from -2 to 2
- attention_moment: float32 [3072, 2048], P(('grp', 'ctx')), may hold values from -48 to 48
- attention_variance: float32 [3072, 2048], P(('grp', 'ctx')), may hold values from 100 to 10000
- swiglu_params: float32 [3072, 3, 2048], P(('grp', 'ctx')), may hold values from -0.125 to 0.125
- swiglu_moment: float32 [3072, 3, 2048], P(('grp', 'ctx')), may hold values from -48 to 48
- swiglu_variance: float32 [3072, 3, 2048], P(('grp', 'ctx')), may hold values from 100 to 10000
- norm_gains: float32 [4352], P(('grp', 'ctx')), may hold values from 0.5 to 2
- gains_moment: float32 [4352], P(('grp', 'ctx')), may hold values from -48 to 48
- gains_variance: float32 [4352], P(('grp', 'ctx')), may hold values from 100 to 10000
Outputs:
- layer_output: bfloat16 [16, 512, 2048], P(('rep', 'grp'), 'ctx')
- hidden_grad: float32 [16, 512, 2048], P(('rep', 'grp'), 'ctx')
- attention_grad: float32 [3072, 2048], P(('grp', 'ctx'))
- swiglu_grad: float32 [3072, 3, 2048], P(('grp', 'ctx'))
- gains_grad: float32 [4352], P(('grp', 'ctx'))
- attention_updated: float32 [3072, 2048], P(('grp', 'ctx'))
- attention_first: float32 [3072, 2048], P(('grp', 'ctx'))
- attention_square: float32 [3072, 2048], P(('grp', 'ctx'))
- swiglu_updated: float32 [3072, 3, 2048], P(('grp', 'ctx'))
- swiglu_first: float32 [3072, 3, 2048], P(('grp', 'ctx'))
- swiglu_square: float32 [3072, 3, 2048], P(('grp', 'ctx'))
- gains_updated: float32 [4352], P(('grp', 'ctx'))
- gains_first: float32 [4352], P(('grp', 'ctx'))
- gains_square: float32 [4352], P(('grp', 'ctx'))
The draws below stay inside these ranges and needn't reach their ends.
Inputs may be any that keep to these rules, and one draw needn't show every extreme that they name: Each sequence's positions are a permutation of 0 to 511 made of runs of 64 consecutive positions, each run starting at a multiple of 64.
All inputs are finite; a program needn't handle non-finite values.
Results may differ from the reference program's by a relative error of at most 0.035.
Values may be sent and summed in bfloat16 or wider, within the bound.
No kernel may reach another device: no remote copies, remote signals or barrier semaphores. Data moves between devices by JAX's collectives and lax.ppermute only.
A program may use at most 512 MiB of HBM per device.

```python
import math
import jax
import jax.numpy as jnp
from jax import lax

D = 2048
QUERY_HEADS = 8
KEY_VALUE_HEADS = 4
HEAD_SIZE = 128
FF = 3072
LEN = 512
PBLOCK = 64
STEP = 4
QW = 1024
KW = 512
ATT_ROWS = 3072
GAINS = 4352
BATCH = 16


def draw_positions(key, part):
    block_count = LEN // PBLOCK
    rank_scores = jax.random.randint(key, (BATCH, block_count), 0, 1048576) * block_count + jnp.arange(block_count)[None, :]
    block_order = jnp.argsort(rank_scores, axis=1, stable=True)
    offsets = jnp.arange(PBLOCK)[None, None, :]
    return (block_order[:, :, None] * PBLOCK + offsets).reshape(BATCH, LEN).astype(jnp.int32)


def draw_attention_params(key, part):
    base_values = jax.random.truncated_normal(key, -4.0, 4.0, (ATT_ROWS, D), jnp.float32)
    row_index = jnp.arange(ATT_ROWS)[:, None]
    scales = jnp.where(row_index >= QW + 2 * KW, 4.0 / math.sqrt(QW), 1.0 / math.sqrt(D))
    return base_values * scales


def level_of(rng, shape, shards, smallest, largest):
    def one(dim, shards_of):
        draws = jax.random.uniform(jax.random.fold_in(jax.random.fold_in(rng, 6), dim), (shards_of,), jnp.float32, smallest / len(shards), largest / len(shards))
        return jnp.repeat(jnp.exp(draws), shape[dim] // shards_of).reshape((-1,) + (1,) * (len(shape) - dim - 1))

    level = one(*shards[0])
    for cut in shards[1:]:
        level = level * one(*cut)
    return level


def bell_draw(key, dims, scale, limit, cuts=(), kind=jnp.bfloat16):
    array = scale * jax.random.normal(key, dims, jnp.float32)
    if cuts:
        array = array * level_of(key, dims, cuts, -0.22, 0.18)
    return jnp.clip(array, -limit, limit).astype(kind)


def setup_inputs(seed: int = 0) -> dict:
    seeds = jax.random.split(jax.random.key(seed), 13)
    hidden = bell_draw(seeds[0], (BATCH, LEN, D), 1.0, 6.0, ((0, 16), (1, 2)))
    positions = draw_positions(jax.random.fold_in(seeds[12], 71), 0)
    cotangent = bell_draw(seeds[2], (BATCH, LEN, D), 1.0, 6.0, ((0, 16), (1, 2)))
    attention_params = draw_attention_params(jax.random.fold_in(seeds[12], 71), 0)
    attention_moment = bell_draw(seeds[4], (ATT_ROWS, D), 8.0, 48.0, ((0, 8),), jnp.float32)
    attention_variance = jnp.clip(jnp.exp(math.log(10000.0) - 4.6051702 * jax.random.uniform(seeds[5], (ATT_ROWS, D), jnp.float32) ** level_of(seeds[5], (ATT_ROWS, D), ((0, 8),), -0.2, 0.2)), 100.0, 10000.0)
    swiglu_params = bell_draw(seeds[6], (FF, 3, D), D ** -0.5, 0.125, ((0, 8),), jnp.float32)
    swiglu_moment = bell_draw(seeds[7], (FF, 3, D), 8.0, 48.0, ((0, 8),), jnp.float32)
    swiglu_variance = jnp.clip(jnp.exp(math.log(10000.0) - 4.6051702 * jax.random.uniform(seeds[8], (FF, 3, D), jnp.float32) ** level_of(seeds[8], (FF, 3, D), ((0, 8),), -0.2, 0.2)), 100.0, 10000.0)
    norm_gains = jnp.clip(0.5 + 1.5 * jax.random.uniform(seeds[9], (GAINS,), jnp.float32) ** level_of(seeds[9], (GAINS,), ((0, 8),), -0.2, 0.2), 0.5, 2.0)
    gains_moment = bell_draw(seeds[10], (GAINS,), 8.0, 48.0, ((0, 8),), jnp.float32)
    gains_variance = jnp.clip(jnp.exp(math.log(10000.0) - 4.6051702 * jax.random.uniform(seeds[11], (GAINS,), jnp.float32) ** level_of(seeds[11], (GAINS,), ((0, 8),), -0.2, 0.2)), 100.0, 10000.0)
    return {"hidden": hidden, "positions": positions, "cotangent": cotangent, "attention_params": attention_params, "attention_moment": attention_moment, "attention_variance": attention_variance, "swiglu_params": swiglu_params, "swiglu_moment": swiglu_moment, "swiglu_variance": swiglu_variance, "norm_gains": norm_gains, "gains_moment": gains_moment, "gains_variance": gains_variance}


EPSILON = 1e-06
THETA = 1000000.0
LEARN = 0.004
BETA_ONE = 0.9
BETA_TWO = 0.95
ADAM_EPSILON = 1e-08
DECAY = 0.1
NEGATIVE = -1e+30

def matmul(left, right):
    return jnp.dot(left, right, preferred_element_type=jnp.float32)

def product_transposed(left, right):
    return lax.dot_general(left, right, (((1,), (1,)), ((), ())), preferred_element_type=jnp.float32)

def matmul_at(left, right):
    return lax.dot_general(left, right, (((0,), (0,)), ((), ())), preferred_element_type=jnp.float32)

def rms_scale(values):
    return lax.rsqrt(lax.optimization_barrier(jnp.mean(values * values, axis=-1, keepdims=True)) + EPSILON)

def rotate_tables(places):
    half_width = HEAD_SIZE // 2
    inverse = jnp.exp(jnp.arange(half_width, dtype=jnp.float32) * (-2.0 * math.log(THETA) / HEAD_SIZE))
    angles = places.astype(jnp.float32)[:, None] * inverse[None, :]
    return (jnp.cos(angles)[:, None, :], jnp.sin(angles)[:, None, :])

def rotate(vectors, cosine_table, sine_table):
    half_width = vectors.shape[-1] // 2
    first_half = vectors[..., :half_width]
    second_half = vectors[..., half_width:]
    return jnp.concatenate([first_half * cosine_table - second_half * sine_table, second_half * cosine_table + first_half * sine_table], axis=-1)

def inverse_rotation(vectors, cosine_table, sine_table):
    half_width = vectors.shape[-1] // 2
    first_half = vectors[..., :half_width]
    second_half = vectors[..., half_width:]
    return jnp.concatenate([first_half * cosine_table + second_half * sine_table, second_half * cosine_table - first_half * sine_table], axis=-1)

def norm_back(upstream, unit_values, scales, gain_vector):
    weighted = upstream * gain_vector
    return scales * (weighted - unit_values * lax.optimization_barrier(jnp.mean(weighted * unit_values, axis=-1, keepdims=True)))

def attention_scores(query_grouped, key_all, place_query, place_key):
    product = jnp.einsum('sqkgd,sckd->skgqc', query_grouped.astype(jnp.float32), key_all.astype(jnp.float32)) * HEAD_SIZE ** (-0.5)
    allowed = place_key[:, None, None, None, :] <= place_query[:, None, None, :, None]
    return jnp.where(allowed, product, NEGATIVE)

def layer_pass(inputs_b, places, cotan, attention_b, swiglu_b, gains_f):
    group_width = QUERY_HEADS // KEY_VALUE_HEADS
    inputs = inputs_b.astype(jnp.float32)
    first_gain = gains_f[:D]
    second_gain = gains_f[D:2 * D]
    query_gain = gains_f[2 * D:2 * D + HEAD_SIZE]
    key_gain = gains_f[2 * D + HEAD_SIZE:]
    w_query = attention_b[:QW]
    key_weight = attention_b[QW:QW + KW]
    w_value = attention_b[QW + KW:QW + 2 * KW]
    w_output = attention_b[QW + 2 * KW:]
    scale_one = rms_scale(inputs)
    unit_one = inputs * scale_one
    first_normed = (unit_one * first_gain).astype(jnp.bfloat16)
    queries = product_transposed(first_normed, w_query).reshape(-1, QUERY_HEADS, HEAD_SIZE)
    local_keys = product_transposed(first_normed, key_weight).reshape(-1, KEY_VALUE_HEADS, HEAD_SIZE)
    local_values = product_transposed(first_normed, w_value)
    query_scale = rms_scale(queries)
    query_unit = queries * query_scale
    key_scale = rms_scale(local_keys)
    key_unit = local_keys * key_scale
    cosine_table, sine_table = rotate_tables(places)
    query_local = rotate(query_unit * query_gain, cosine_table, sine_table).astype(jnp.bfloat16)
    key_local = rotate(key_unit * key_gain, cosine_table, sine_table).astype(jnp.bfloat16)
    value_local = local_values.astype(jnp.bfloat16).reshape(-1, KEY_VALUE_HEADS, HEAD_SIZE)
    query_grouped = query_local.reshape(1, -1, KEY_VALUE_HEADS, group_width, HEAD_SIZE)
    key_all = key_local[None]
    value_all = value_local[None]
    scores = attention_scores(query_grouped, key_all, places[None], places[None])
    top_score = lax.optimization_barrier(jnp.max(scores, axis=-1, keepdims=True))
    log_total = top_score + jnp.log(lax.optimization_barrier(jnp.sum(jnp.exp(scores - top_score), axis=-1, keepdims=True)))
    attention_probs = jnp.exp(scores - log_total)
    probs_b = attention_probs.astype(jnp.bfloat16)
    mixed_b = jnp.einsum('skgqc,sckd->sqkgd', probs_b.astype(jnp.float32), value_all.astype(jnp.float32)).astype(jnp.bfloat16)
    mixed_rows = mixed_b.reshape(-1, QW)
    residual = inputs + matmul(mixed_rows, w_output)
    scale_two = rms_scale(residual)
    unit_two = residual * scale_two
    normed_two = (unit_two * second_gain).astype(jnp.bfloat16)
    w_gate = swiglu_b[:, 0]
    w_up = swiglu_b[:, 1]
    w_down = swiglu_b[:, 2]
    gate_values = product_transposed(normed_two, w_gate)
    up_values = product_transposed(normed_two, w_up)
    sigmoid_gate = jax.nn.sigmoid(gate_values)
    active = gate_values * sigmoid_gate
    hidden_b = (active * up_values).astype(jnp.bfloat16)
    layer_sum = residual + matmul(hidden_b, w_down)
    layer_output = layer_sum.astype(jnp.bfloat16)
    d_hidden = product_transposed(cotan, w_down)
    grad_down = matmul_at(hidden_b, cotan)
    d_gate = (d_hidden * up_values * sigmoid_gate * (1.0 + gate_values * (1.0 - sigmoid_gate))).astype(jnp.bfloat16)
    d_upper = (d_hidden * active).astype(jnp.bfloat16)
    d_normed_two = matmul(d_gate, w_gate) + matmul(d_upper, w_up)
    grad_gate = matmul_at(d_gate, normed_two)
    grad_up = matmul_at(d_upper, normed_two)
    grad_second = lax.optimization_barrier(jnp.sum(d_normed_two * unit_two, axis=0))
    d_residual = cotan.astype(jnp.float32) + norm_back(d_normed_two, unit_two, scale_two, second_gain)
    d_residual_b = d_residual.astype(jnp.bfloat16)
    mixed_gradient_local = product_transposed(d_residual_b, w_output).astype(jnp.bfloat16)
    grad_output = matmul_at(mixed_rows, d_residual_b)
    mixed_gradient_grouped = mixed_gradient_local.reshape(1, -1, KEY_VALUE_HEADS, group_width, HEAD_SIZE)
    row_delta = lax.optimization_barrier(jnp.sum(mixed_gradient_grouped.astype(jnp.float32) * mixed_b.astype(jnp.float32), axis=-1))
    row_delta = jnp.transpose(row_delta, (0, 2, 3, 1))[..., None]
    d_probs = jnp.einsum('sqkgd,sckd->skgqc', mixed_gradient_grouped.astype(jnp.float32), value_all.astype(jnp.float32))
    d_scores = (attention_probs * (d_probs - row_delta) * HEAD_SIZE ** (-0.5)).astype(jnp.bfloat16)
    d_query = jnp.einsum('skgqc,sckd->sqkgd', d_scores.astype(jnp.float32), key_all.astype(jnp.float32)).reshape(-1, QUERY_HEADS, HEAD_SIZE)
    key_gradient = jnp.einsum('skgqc,sqkgd->sckd', d_scores.astype(jnp.float32), query_grouped.astype(jnp.float32))[0]
    d_value = jnp.einsum('skgqc,sqkgd->sckd', probs_b.astype(jnp.float32), mixed_gradient_grouped.astype(jnp.float32))[0]
    d_query_unit = inverse_rotation(d_query, cosine_table, sine_table)
    grad_query_gain = lax.optimization_barrier(jnp.sum(d_query_unit * query_unit, axis=(0, 1)))
    d_query_b = norm_back(d_query_unit, query_unit, query_scale, query_gain).astype(jnp.bfloat16).reshape(-1, QW)
    unit_key_gradient = inverse_rotation(key_gradient, cosine_table, sine_table)
    grad_key_gain = lax.optimization_barrier(jnp.sum(unit_key_gradient * key_unit, axis=(0, 1)))
    d_key_b = norm_back(unit_key_gradient, key_unit, key_scale, key_gain).astype(jnp.bfloat16).reshape(-1, KW)
    d_value_b = d_value.reshape(-1, KW).astype(jnp.bfloat16)
    d_normed_one = matmul(d_query_b, w_query) + matmul(d_key_b, key_weight) + matmul(d_value_b, w_value)
    grad_first = lax.optimization_barrier(jnp.sum(d_normed_one * unit_one, axis=0))
    hidden_grad = d_residual + norm_back(d_normed_one, unit_one, scale_one, first_gain)
    attention_grad = jnp.concatenate([matmul_at(d_query_b, first_normed), matmul_at(d_key_b, first_normed), matmul_at(d_value_b, first_normed), grad_output], axis=0)
    swiglu_grad = jnp.stack([grad_gate, grad_up, grad_down], axis=1)
    gains_grad = jnp.concatenate([grad_first, grad_second, grad_query_gain, grad_key_gain])
    return (layer_output, hidden_grad, attention_grad, swiglu_grad, gains_grad)

def adam_update(params, moment, variance, gradient, decay_rate):
    first = BETA_ONE * moment + (1.0 - BETA_ONE) * gradient
    square = BETA_TWO * variance + (1.0 - BETA_TWO) * gradient * gradient
    corrected = first / (1.0 - BETA_ONE ** STEP)
    spread = jnp.sqrt(square / (1.0 - BETA_TWO ** STEP)) + ADAM_EPSILON
    updated = params - LEARN * (corrected / spread + decay_rate * params)
    return (updated, first, square)

def reference(hidden, positions, cotangent, attention_params, attention_moment, attention_variance, swiglu_params, swiglu_moment, swiglu_variance, norm_gains, gains_moment, gains_variance):
    attention_b = attention_params.astype(jnp.bfloat16)
    swiglu_b = swiglu_params.astype(jnp.bfloat16)
    gains_f = lax.optimization_barrier(norm_gains.astype(jnp.bfloat16)).astype(jnp.float32)

    def accumulate(running, sample):
        result = layer_pass(sample[0], sample[1], sample[2], attention_b, swiglu_b, gains_f)
        return ((running[0] + result[2], running[1] + result[3], running[2] + result[4]), (result[0], result[1]))
    start_sums = (jnp.zeros(attention_params.shape, jnp.float32), jnp.zeros(swiglu_params.shape, jnp.float32), jnp.zeros(norm_gains.shape, jnp.float32))
    totals, produced = lax.scan(accumulate, start_sums, (hidden, positions, cotangent))
    attention_new = adam_update(attention_params, attention_moment, attention_variance, totals[0], DECAY)
    swiglu_new = adam_update(swiglu_params, swiglu_moment, swiglu_variance, totals[1], DECAY)
    gains_new = adam_update(norm_gains, gains_moment, gains_variance, totals[2], 0.0)
    return (produced[0], produced[1], totals[0], totals[1], totals[2], attention_new[0], attention_new[1], attention_new[2], swiglu_new[0], swiglu_new[1], swiglu_new[2], gains_new[0], gains_new[1], gains_new[2])
```

```python
import math

import jax
import jax.numpy as jnp
from jax import lax
from jax.sharding import PartitionSpec as P

QUERY_HEADS = 8
KEY_VALUE_HEADS = 4
HEAD_SIZE = 128
STEP = 4
QW = 1024
KW = 512


EPSILON = 1e-06
THETA = 1000000.0
LEARN = 0.004
BETA_ONE = 0.9
BETA_TWO = 0.95
ADAM_EPSILON = 1e-08
DECAY = 0.1
NEGATIVE = -1e30


def matmul(left, right):
    return jnp.dot(left, right, preferred_element_type=jnp.float32)


def product_transposed(left, right):
    return lax.dot_general(
        left, right, (((1,), (1,)), ((), ())), preferred_element_type=jnp.float32
    )


def matmul_at(left, right):
    return lax.dot_general(
        left, right, (((0,), (0,)), ((), ())), preferred_element_type=jnp.float32
    )


def rms_scale(values):
    return lax.rsqrt(jnp.mean(values * values, axis=-1, keepdims=True) + EPSILON)


def rotate_tables(places):
    half_width = HEAD_SIZE // 2
    inverse = jnp.exp(
        jnp.arange(half_width, dtype=jnp.float32) * (-2.0 * math.log(THETA) / HEAD_SIZE)
    )
    angles = places.astype(jnp.float32)[:, None] * inverse[None, :]
    return (jnp.cos(angles)[:, None, :], jnp.sin(angles)[:, None, :])


def rotate(vectors, cosine_table, sine_table):
    half_width = vectors.shape[-1] // 2
    first_half = vectors[..., :half_width]
    second_half = vectors[..., half_width:]
    return jnp.concatenate(
        [
            first_half * cosine_table - second_half * sine_table,
            second_half * cosine_table + first_half * sine_table,
        ],
        axis=-1,
    )


def inverse_rotation(vectors, cosine_table, sine_table):
    half_width = vectors.shape[-1] // 2
    first_half = vectors[..., :half_width]
    second_half = vectors[..., half_width:]
    return jnp.concatenate(
        [
            first_half * cosine_table + second_half * sine_table,
            second_half * cosine_table - first_half * sine_table,
        ],
        axis=-1,
    )


def norm_back(upstream, unit_values, scales, gain_vector):
    weighted = upstream * gain_vector
    return scales * (
        weighted - unit_values * jnp.mean(weighted * unit_values, axis=-1, keepdims=True)
    )


def attention_scores(query_grouped, key_all, place_query, place_key):
    product = jnp.einsum(
        "sqkgd,sckd->skgqc", query_grouped, key_all, preferred_element_type=jnp.float32
    ) * HEAD_SIZE ** (-0.5)
    allowed = place_key[:, None, None, None, :] <= place_query[:, None, None, :, None]
    return jnp.where(allowed, product, NEGATIVE)


def gate_forward(normed_rows, w_gate, w_up):
    gate_values = product_transposed(normed_rows, w_gate)
    up_values = product_transposed(normed_rows, w_up)
    sigmoid_gate = jax.nn.sigmoid(gate_values)
    active = gate_values * sigmoid_gate
    hidden_b = (active * up_values).astype(jnp.bfloat16)
    return (gate_values, up_values, sigmoid_gate, active, hidden_b)


def gate_backward(d_hidden, gate_values, up_values, sigmoid_gate, active):
    d_gate = (
        d_hidden * up_values * sigmoid_gate * (1.0 + gate_values * (1.0 - sigmoid_gate))
    ).astype(jnp.bfloat16)
    d_upper = (d_hidden * active).astype(jnp.bfloat16)
    return (d_gate, d_upper)


def adam_update(params, moment, variance, gradient, decay_rate):
    first = BETA_ONE * moment + (1.0 - BETA_ONE) * gradient
    square = BETA_TWO * variance + (1.0 - BETA_TWO) * gradient * gradient
    corrected = first / (1.0 - BETA_ONE**STEP)
    spread = jnp.sqrt(square / (1.0 - BETA_TWO**STEP)) + ADAM_EPSILON
    updated = params - LEARN * (corrected / spread + decay_rate * params)
    return (updated, first, square)


def rounded(values):
    return values.astype(jnp.bfloat16)


def widened(values):
    return values.astype(jnp.float32)


def added(left, right):
    return rounded(widened(left) + widened(right))


def build(mesh):
    rep_size = mesh.shape["rep"]
    grp_size = mesh.shape["grp"]
    pair = 2 if rep_size % 2 == 0 else 1
    lanes = rep_size // pair
    plus_steps = grp_size // 2
    minus_steps = grp_size - 1 - plus_steps

    def core_swap(values):
        return lax.ppermute(values, "rep", [(i, i ^ 1) for i in range(rep_size)])

    def lane_swap(values, offset):
        return lax.ppermute(values, "rep", [(i, i ^ (offset * pair)) for i in range(rep_size)])

    def ctx_swap(values):
        return lax.ppermute(values, "ctx", [(0, 1), (1, 0)])

    def grp_shift(values, offset):
        return lax.ppermute(
            values, "grp", [(i, (i + offset) % grp_size) for i in range(grp_size)]
        )

    def grp_gather(block, after=None):
        blocks = {0: block}
        first = block
        if after is not None:
            first = lax.optimization_barrier((block, after))[0]
        current = first
        for step in range(1, plus_steps + 1):
            current = grp_shift(current, 1)
            blocks[step] = current
        current = first
        for step in range(1, minus_steps + 1):
            current = grp_shift(current, -1)
            blocks[grp_size - step] = current
        return blocks

    reduce_order = (
        list(range(plus_steps, 0, -1))
        + list(range(plus_steps + 1, grp_size))
        + [0]
    )

    class GrpReduce:
        def __init__(self):
            self.low = None
            self.high = None

        def push(self, k, block):
            if k == 0:
                total = widened(block)
                for part in (self.low, self.high):
                    if part is not None:
                        total = total + widened(part)
                return total
            if k <= plus_steps:
                if self.low is not None:
                    block = added(block, self.low)
                self.low = grp_shift(block, -1)
            else:
                if self.high is not None:
                    block = added(block, self.high)
                self.high = grp_shift(block, 1)
            return None

    def all_sum(values):
        for bit in range((rep_size - 1).bit_length()):
            values = values + lax.ppermute(
                values, "rep", [(i, i ^ (1 << bit)) for i in range(rep_size)]
            )
        values = values + ctx_swap(values)
        for bit in range((grp_size - 1).bit_length()):
            values = values + lax.ppermute(
                values, "grp", [(i, i ^ (1 << bit)) for i in range(grp_size)]
            )
        return values

    def shards(
        hidden,
        positions,
        cotangent,
        attention_params,
        attention_moment,
        attention_variance,
        swiglu_params,
        swiglu_moment,
        swiglu_variance,
        norm_gains,
        gains_moment,
        gains_variance,
    ):
        sequence_count, token_count, model_width = hidden.shape
        row_number = sequence_count * token_count
        group_width = QUERY_HEADS // KEY_VALUE_HEADS
        rep_at = lax.axis_index("rep")
        grp_at = lax.axis_index("grp")
        ctx_at = lax.axis_index("ctx")
        core_at = rep_at % pair

        gain_rows = norm_gains.shape[0]
        gains_pair = rounded(norm_gains)[None]
        gains_other = ctx_swap(gains_pair)
        both = jnp.where(
            ctx_at == 0,
            jnp.concatenate([gains_pair, gains_other]),
            jnp.concatenate([gains_other, gains_pair]),
        )
        gains_all = jnp.zeros((grp_size, 2, gain_rows), jnp.bfloat16)
        for k in range(grp_size):
            arrived = both if k == 0 else grp_shift(both, k)
            gains_all = lax.dynamic_update_slice(
                gains_all, arrived[None], ((grp_at - k) % grp_size, 0, 0)
            )
        gains_f = widened(gains_all.reshape(-1))
        first_gain = gains_f[:model_width]
        second_gain = gains_f[model_width : 2 * model_width]
        query_gain = gains_f[2 * model_width : 2 * model_width + HEAD_SIZE]
        key_gain = gains_f[2 * model_width + HEAD_SIZE :]

        att_rows = attention_params.shape[0]
        half_rows = att_rows // pair
        attention_own = rounded(attention_params)
        half_own = lax.dynamic_slice_in_dim(attention_own, core_at * half_rows, half_rows, 0)
        near = grp_gather(half_own)
        last_near = near[plus_steps]
        attention_all = jnp.zeros((grp_size, 2, pair, half_rows, model_width), jnp.bfloat16)

        def place(buffer, values, k, plane, core):
            return lax.dynamic_update_slice(
                buffer,
                values[None, None, None],
                ((grp_at - k) % grp_size, ctx_at ^ plane, core_at ^ core, 0, 0),
            )

        attention_all = lax.dynamic_update_slice(
            attention_all,
            attention_own.reshape(1, 1, pair, half_rows, model_width),
            (grp_at, ctx_at, 0, 0, 0),
        )
        for k in range(grp_size):
            far = ctx_swap(near[k])
            attention_all = place(attention_all, far, k, 1, 0)
            if k:
                attention_all = place(attention_all, near[k], k, 0, 0)
            if pair == 2:
                attention_all = place(attention_all, core_swap(far), k, 1, 1)
                if k:
                    attention_all = place(attention_all, core_swap(near[k]), k, 0, 1)
        attention_all = attention_all.reshape(-1, model_width)

        cotan_rows = cotangent.reshape(row_number, model_width)
        cotan_both = jnp.concatenate([cotan_rows, ctx_swap(cotan_rows)])

        units = swiglu_params.shape[0]
        piece = units // rep_size
        swiglu_t = jnp.transpose(swiglu_params, (1, 0, 2))

        def own_piece(offset):
            return rounded(
                lax.dynamic_slice_in_dim(swiglu_t, (rep_at ^ offset) * piece, piece, 1)
            )

        ring = grp_gather(own_piece(0), after=last_near)
        weights = [jnp.zeros((grp_size * units, model_width), jnp.bfloat16) for _ in range(3)]

        def put(values, k, core, lane):
            start = k * units + (core * lanes + lane) * piece
            for j in range(3):
                weights[j] = lax.dynamic_update_slice(weights[j], values[j], (start, 0))

        for k in range(grp_size):
            for lane in range(lanes):
                if k == 0:
                    for core in range(pair):
                        put(own_piece(lane * pair + core), k, core, lane)
                    continue
                arrived = ring[k] if lane == 0 else lane_swap(ring[k], lane)
                put(arrived, k, 0, lane)
                if pair == 2:
                    put(core_swap(arrived), k, 1, lane)
        w_gate, w_up, w_down = weights

        w_output = attention_all[QW + 2 * KW :]
        w_qkv = attention_all[: QW + 2 * KW]
        start_row = ctx_at * token_count
        places_own = lax.dynamic_slice_in_dim(positions, start_row, token_count, 1)
        places_far = lax.dynamic_slice_in_dim(
            positions, (1 - ctx_at) * token_count, token_count, 1
        )
        places_all = jnp.concatenate([places_own, places_far], axis=1)
        inputs = widened(hidden.reshape(row_number, model_width))
        scale_one = rms_scale(inputs)
        unit_one = inputs * scale_one
        first_normed = rounded(unit_one * first_gain)
        projected = product_transposed(first_normed, w_qkv)
        queries = projected[:, :QW].reshape(row_number, QUERY_HEADS, HEAD_SIZE)
        local_keys = projected[:, QW : QW + KW].reshape(row_number, KEY_VALUE_HEADS, HEAD_SIZE)
        local_values = projected[:, QW + KW :]
        query_scale = rms_scale(queries)
        query_unit = queries * query_scale
        key_scale = rms_scale(local_keys)
        key_unit = local_keys * key_scale
        cosine_table, sine_table = rotate_tables(places_own.reshape(-1))
        query_local = rounded(rotate(query_unit * query_gain, cosine_table, sine_table))
        key_local = rounded(rotate(key_unit * key_gain, cosine_table, sine_table))
        key_value = jnp.concatenate(
            [key_local.reshape(row_number, KW), rounded(local_values)], axis=1
        )
        key_value_far = ctx_swap(key_value)

        def over_sequence(first, count):
            own = key_value[:, first : first + count]
            far = key_value_far[:, first : first + count]
            shape = (sequence_count, token_count, KEY_VALUE_HEADS, HEAD_SIZE)
            return jnp.concatenate([own.reshape(shape), far.reshape(shape)], axis=1)

        key_all = over_sequence(0, KW)
        value_all = over_sequence(KW, KW)
        query_grouped = query_local.reshape(
            sequence_count, token_count, KEY_VALUE_HEADS, group_width, HEAD_SIZE
        )
        scores = attention_scores(query_grouped, key_all, places_own, places_all)
        top_score = jnp.max(scores, axis=-1, keepdims=True)
        log_total = top_score + jnp.log(
            jnp.sum(jnp.exp(scores - top_score), axis=-1, keepdims=True)
        )
        probs = jnp.exp(scores - log_total)
        probs_b = rounded(probs)
        mixed_b = rounded(
            jnp.einsum(
                "skgqc,sckd->sqkgd", probs_b, value_all, preferred_element_type=jnp.float32
            )
        )
        mixed_rows = mixed_b.reshape(row_number, QW)
        residual = inputs + matmul(mixed_rows, w_output)
        scale_two = rms_scale(residual)
        unit_two = residual * scale_two
        normed_two = rounded(unit_two * second_gain)
        normed_both = jnp.concatenate([normed_two, ctx_swap(normed_two)])

        gate_values, up_values, sigmoid_gate, active, hidden_b = gate_forward(
            normed_both, w_gate, w_up
        )
        d_hidden = product_transposed(cotan_both, w_down)
        d_gate, d_upper = gate_backward(d_hidden, gate_values, up_values, sigmoid_gate, active)
        d_normed_both = matmul(d_gate, w_gate) + matmul(d_upper, w_up)
        d_normed_two = d_normed_both[:row_number] + widened(
            ctx_swap(rounded(d_normed_both[row_number:]))
        )
        layer_both = matmul(hidden_b, w_down)
        layer_sum = (residual + layer_both[:row_number]) + widened(
            ctx_swap(rounded(layer_both[row_number:]))
        )
        layer_output = rounded(layer_sum).reshape(sequence_count, token_count, model_width)

        half_units = units // pair
        reducer = GrpReduce()
        swiglu_piece = None
        for k in reduce_order:

            def half(core):
                lo = k * units + core * half_units
                cols = slice(lo, lo + half_units)
                return [
                    rounded(matmul_at(d_gate[:, cols], normed_both)),
                    rounded(matmul_at(d_upper[:, cols], normed_both)),
                    rounded(matmul_at(hidden_b[:, cols], cotan_both)),
                ]

            if pair == 2:
                sent = [core_swap(part) for part in half(1)]
                kept = half(0)
                parts = [(a, b) for a, b in zip(kept, sent)]
            else:
                parts = [(a,) for a in half(0)]

            def lane_block(lane):
                rows = slice(lane * piece, (lane + 1) * piece)
                return jnp.stack([sum(widened(p[rows]) for p in part) for part in parts])

            total = lane_block(0)
            for lane in range(1, lanes):
                total = total + widened(lane_swap(rounded(lane_block(lane)), lane))
            swiglu_piece = reducer.push(k, rounded(total))
        swiglu_piece = rounded(swiglu_piece)

        def spread(values, axis):
            blocks = {}
            for lane in range(lanes):
                blocks[lane * pair] = values if lane == 0 else lane_swap(values, lane)
                if pair == 2:
                    blocks[lane * pair + 1] = core_swap(blocks[lane * pair])
            count = values.shape[axis]
            shape = list(values.shape)
            shape[axis] = count * rep_size
            result = jnp.zeros(shape, values.dtype)
            for offset, block in blocks.items():
                result = lax.dynamic_update_slice_in_dim(
                    result, block, (rep_at ^ offset) * count, axis
                )
            return result

        swiglu_grad = jnp.transpose(widened(spread(swiglu_piece, 1)), (1, 0, 2))

        grad_second = jnp.sum(d_normed_two * unit_two, axis=0)
        d_residual = widened(cotan_rows) + norm_back(d_normed_two, unit_two, scale_two, second_gain)
        d_residual_b = rounded(d_residual)
        mixed_gradient_local = rounded(product_transposed(d_residual_b, w_output))
        grad_output = rounded(matmul_at(mixed_rows, d_residual_b))
        mixed_gradient_grouped = mixed_gradient_local.reshape(
            sequence_count, token_count, KEY_VALUE_HEADS, group_width, HEAD_SIZE
        )
        row_delta = jnp.sum(widened(mixed_gradient_grouped) * widened(mixed_b), axis=-1)
        row_delta = jnp.transpose(row_delta, (0, 2, 3, 1))[..., None]
        d_probs = jnp.einsum(
            "sqkgd,sckd->skgqc",
            mixed_gradient_grouped,
            value_all,
            preferred_element_type=jnp.float32,
        )
        d_scores = rounded(probs * (d_probs - row_delta) * HEAD_SIZE ** (-0.5))
        d_query = jnp.einsum(
            "skgqc,sckd->sqkgd", d_scores, key_all, preferred_element_type=jnp.float32
        ).reshape(row_number, QUERY_HEADS, HEAD_SIZE)
        d_key_all = jnp.einsum(
            "skgqc,sqkgd->sckd", d_scores, query_grouped, preferred_element_type=jnp.float32
        )
        d_value_all = jnp.einsum(
            "skgqc,sqkgd->sckd",
            probs_b,
            mixed_gradient_grouped,
            preferred_element_type=jnp.float32,
        )
        d_key_value = jnp.concatenate(
            [
                d_key_all.reshape(sequence_count, 2, token_count, KW),
                d_value_all.reshape(sequence_count, 2, token_count, KW),
            ],
            axis=-1,
        )
        d_key_value = d_key_value[:, 0] + widened(ctx_swap(rounded(d_key_value[:, 1])))
        d_key_value = d_key_value.reshape(row_number, 2 * KW)
        key_gradient = d_key_value[:, :KW]
        d_value_b = rounded(d_key_value[:, KW:])
        d_query_unit = inverse_rotation(d_query, cosine_table, sine_table)
        grad_query_gain = jnp.sum(d_query_unit * query_unit, axis=(0, 1))
        d_query_b = rounded(
            norm_back(d_query_unit, query_unit, query_scale, query_gain)
        ).reshape(row_number, QW)
        unit_key_gradient = inverse_rotation(
            key_gradient.reshape(row_number, KEY_VALUE_HEADS, HEAD_SIZE), cosine_table, sine_table
        )
        grad_key_gain = jnp.sum(unit_key_gradient * key_unit, axis=(0, 1))
        d_key_b = rounded(norm_back(unit_key_gradient, key_unit, key_scale, key_gain)).reshape(
            row_number, KW
        )
        d_qkv = jnp.concatenate([d_query_b, d_key_b, d_value_b], axis=1)
        attention_full = jnp.concatenate(
            [rounded(matmul_at(d_qkv, first_normed)), grad_output], axis=0
        ).reshape(grp_size, 2, pair, half_rows, model_width)

        def block_of(k, plane, core):
            return lax.dynamic_slice(
                attention_full,
                ((grp_at - k) % grp_size, ctx_at ^ plane, core_at ^ core, 0, 0),
                (1, 1, 1, half_rows, model_width),
            ).reshape(half_rows, model_width)

        reducer = GrpReduce()
        attention_half = None
        for k in reduce_order:
            own, far = block_of(k, 0, 0), block_of(k, 1, 0)
            if pair == 2:
                far = added(far, core_swap(block_of(k, 1, 1)))
                own = widened(own) + widened(core_swap(block_of(k, 0, 1)))
            attention_half = reducer.push(k, added(own, ctx_swap(far)))
        attention_half = rounded(attention_half)
        bit = 1
        while bit < lanes:
            attention_half = added(attention_half, lane_swap(attention_half, bit))
            bit *= 2
        attention_grad = attention_half
        if pair == 2:
            attention_grad = jnp.zeros((att_rows, model_width), jnp.bfloat16)
            for core, block in ((0, attention_half), (1, core_swap(attention_half))):
                attention_grad = lax.dynamic_update_slice(
                    attention_grad, block, ((core_at ^ core) * half_rows, 0)
                )
        attention_grad = widened(attention_grad)

        d_normed_one = matmul(d_qkv, w_qkv)
        grad_first = jnp.sum(d_normed_one * unit_one, axis=0)
        hidden_grad = d_residual + norm_back(d_normed_one, unit_one, scale_one, first_gain)
        gains_total = all_sum(
            jnp.concatenate([grad_first, grad_second, grad_query_gain, grad_key_gain])
        )
        gains_grad = lax.dynamic_slice_in_dim(
            gains_total, (grp_at * 2 + ctx_at) * gain_rows, gain_rows, 0
        )
        attention_new = adam_update(
            attention_params, attention_moment, attention_variance, attention_grad, DECAY
        )
        swiglu_new = adam_update(
            swiglu_params, swiglu_moment, swiglu_variance, swiglu_grad, DECAY
        )
        gains_new = adam_update(norm_gains, gains_moment, gains_variance, gains_grad, 0.0)
        return (
            layer_output,
            hidden_grad.reshape(sequence_count, token_count, model_width),
            attention_grad,
            swiglu_grad,
            gains_grad,
            attention_new[0],
            attention_new[1],
            attention_new[2],
            swiglu_new[0],
            swiglu_new[1],
            swiglu_new[2],
            gains_new[0],
            gains_new[1],
            gains_new[2],
        )

    return shards


def solution(mesh):
    in_specs = (
        P(("rep", "grp"), "ctx", None),
        P(("rep", "grp"), None),
        P(("rep", "grp"), "ctx", None),
        P(("grp", "ctx"), None),
        P(("grp", "ctx"), None),
        P(("grp", "ctx"), None),
        P(("grp", "ctx"), None, None),
        P(("grp", "ctx"), None, None),
        P(("grp", "ctx"), None, None),
        P(("grp", "ctx")),
        P(("grp", "ctx")),
        P(("grp", "ctx")),
    )
    out_specs = (
        P(("rep", "grp"), "ctx", None),
        P(("rep", "grp"), "ctx", None),
        P(("grp", "ctx"), None),
        P(("grp", "ctx"), None, None),
        P(("grp", "ctx")),
        P(("grp", "ctx"), None),
        P(("grp", "ctx"), None),
        P(("grp", "ctx"), None),
        P(("grp", "ctx"), None, None),
        P(("grp", "ctx"), None, None),
        P(("grp", "ctx"), None, None),
        P(("grp", "ctx")),
        P(("grp", "ctx")),
        P(("grp", "ctx")),
    )
    return jax.shard_map(
        build(mesh), mesh=mesh, in_specs=in_specs, out_specs=out_specs, check_vma=False
    )
```

```python
import math

import jax
import jax.numpy as jnp
from jax import lax
from jax.experimental import pallas as pl
from jax.experimental.pallas import tpu as pltpu
from jax.sharding import PartitionSpec as P

QUERY_HEADS = 8
KEY_VALUE_HEADS = 4
HEAD_SIZE = 128
STEP = 4
QW = 1024
KW = 512


EPSILON = 1e-06
THETA = 1000000.0
LEARN = 0.004
BETA_ONE = 0.9
BETA_TWO = 0.95
ADAM_EPSILON = 1e-08
DECAY = 0.1
NEGATIVE = -1e30


def matmul(left, right):
    return jnp.dot(left, right, preferred_element_type=jnp.float32)


def product_transposed(left, right):
    return lax.dot_general(
        left, right, (((1,), (1,)), ((), ())), preferred_element_type=jnp.float32
    )


def matmul_at(left, right):
    return lax.dot_general(
        left, right, (((0,), (0,)), ((), ())), preferred_element_type=jnp.float32
    )


def rms_scale(values):
    return lax.rsqrt(jnp.mean(values * values, axis=-1, keepdims=True) + EPSILON)


def rotate_tables(places):
    half_width = HEAD_SIZE // 2
    inverse = jnp.exp(
        jnp.arange(half_width, dtype=jnp.float32) * (-2.0 * math.log(THETA) / HEAD_SIZE)
    )
    angles = places.astype(jnp.float32)[:, None] * inverse[None, :]
    cosine, sine = jnp.cos(angles), jnp.sin(angles)
    return (
        jnp.concatenate([cosine, cosine], axis=-1),
        jnp.concatenate([-sine, sine], axis=-1),
    )


def norm_back(upstream, unit_values, scales, gain_vector):
    weighted = upstream * gain_vector
    return scales * (
        weighted - unit_values * jnp.mean(weighted * unit_values, axis=-1, keepdims=True)
    )


def gate_forward(normed_rows, w_gate, w_up):
    gate_values = product_transposed(normed_rows, w_gate)
    up_values = product_transposed(normed_rows, w_up)
    sigmoid_gate = jax.nn.sigmoid(gate_values)
    active = gate_values * sigmoid_gate
    hidden_b = (active * up_values).astype(jnp.bfloat16)
    return (gate_values, up_values, sigmoid_gate, active, hidden_b)


def gate_backward(d_hidden, gate_values, up_values, sigmoid_gate, active):
    d_gate = (
        d_hidden * up_values * sigmoid_gate * (1.0 + gate_values * (1.0 - sigmoid_gate))
    ).astype(jnp.bfloat16)
    d_upper = (d_hidden * active).astype(jnp.bfloat16)
    return (d_gate, d_upper)


def adam_update(params, moment, variance, gradient, decay_rate):
    first = BETA_ONE * moment + (1.0 - BETA_ONE) * gradient
    square = BETA_TWO * variance + (1.0 - BETA_TWO) * gradient * gradient
    corrected = first / (1.0 - BETA_ONE**STEP)
    spread = jnp.sqrt(square / (1.0 - BETA_TWO**STEP)) + ADAM_EPSILON
    updated = params - LEARN * (corrected / spread + decay_rate * params)
    return (updated, first, square)


def rounded(values):
    return values.astype(jnp.bfloat16)


def widened(values):
    return values.astype(jnp.float32)


def added(left, right):
    return rounded(widened(left) + widened(right))


def tie(value, *others):
    return lax.optimization_barrier((value,) + others)[0]


def copied_into(buffers, shapes, where, copies):
    sources = [source for source, _, _, _ in copies]
    count = len(shapes)
    offset = count if buffers else 0

    def body(where_ref, *refs):
        inputs = refs[offset : offset + len(copies)]
        outputs = refs[offset + len(copies) : offset + len(copies) + count]
        semaphores = refs[-1]
        started = []
        for number, (_, target, place, part) in enumerate(copies):
            source = inputs[number]
            if part is not None:
                source = source.at[part]
            copy = pltpu.make_async_copy(
                source, outputs[target].at[place(where_ref)], semaphores.at[number]
            )
            copy.start()
            started.append(copy)
        for copy in started:
            copy.wait()

    anywhere = pl.BlockSpec(memory_space=pl.ANY)
    return pl.pallas_call(
        body,
        in_specs=[pl.BlockSpec(memory_space=pltpu.SMEM)] + [anywhere] * (offset + len(copies)),
        out_specs=[anywhere] * count,
        out_shape=[jax.ShapeDtypeStruct(shape, jnp.bfloat16) for shape in shapes],
        scratch_shapes=[pltpu.SemaphoreType.DMA((len(copies),))],
        input_output_aliases={1 + i: i for i in range(offset)},
    )(where, *(buffers or []), *sources)


def head_slice(index):
    return slice(index * HEAD_SIZE, (index + 1) * HEAD_SIZE)


def swapped(values):
    return pltpu.roll(values, HEAD_SIZE // 2, 1)


def project(rows, weights, cosine, sine, gain_table, first, last):
    count, width = rows.shape
    block = 2 * HEAD_SIZE
    total = last - first
    skip = first // block
    rotated_blocks = (QW + KW) // block - skip

    def body(x_ref, w_ref, c_ref, s_ref, g_ref, lin_ref, out_ref):
        lin = product_transposed(x_ref[...], w_ref[...])
        lin_ref[...] = lin
        step = pl.program_id(0)

        @pl.when(step < rotated_blocks)
        def _():
            for h in range(2):
                part = lin[:, head_slice(h)]
                part = part * rms_scale(part) * g_ref[0]
                out_ref[:, head_slice(h)] = rounded(
                    part * c_ref[...] + swapped(part) * s_ref[...]
                )

        @pl.when(step >= rotated_blocks)
        def _():
            out_ref[...] = rounded(lin)

    return pl.pallas_call(
        body,
        grid=(total // block,),
        in_specs=[
            pl.BlockSpec((count, width), lambda i: (0, 0)),
            pl.BlockSpec((block, width), lambda i: (skip + i, 0)),
            pl.BlockSpec((count, HEAD_SIZE), lambda i: (0, 0)),
            pl.BlockSpec((count, HEAD_SIZE), lambda i: (0, 0)),
            pl.BlockSpec((1, 1, HEAD_SIZE), lambda i: (skip + i, 0, 0)),
        ],
        out_specs=[
            pl.BlockSpec((count, block), lambda i: (0, i)),
            pl.BlockSpec((count, block), lambda i: (0, i)),
        ],
        out_shape=[
            jax.ShapeDtypeStruct((count, total), jnp.float32),
            jax.ShapeDtypeStruct((count, total), jnp.bfloat16),
        ],
    )(rows, weights, cosine, sine, gain_table)


def pair_probs(query, keys, allowed):
    scores = [
        jnp.where(mask, product_transposed(query, key) * HEAD_SIZE ** (-0.5), NEGATIVE)
        for key, mask in zip(keys, allowed)
    ]
    top = jnp.maximum(*[jnp.max(s, axis=-1, keepdims=True) for s in scores])
    powers = [jnp.exp(s - top) for s in scores]
    total = sum(jnp.sum(p, axis=-1, keepdims=True) for p in powers)
    return [p * (1.0 / total) for p in powers]


def attention_specs(count):
    heads = QUERY_HEADS // KEY_VALUE_HEADS * HEAD_SIZE
    return [
        pl.BlockSpec((count, heads), lambda i: (0, i)),
        pl.BlockSpec((count, HEAD_SIZE), lambda i: (0, i)),
        pl.BlockSpec((count, HEAD_SIZE), lambda i: (0, KEY_VALUE_HEADS + i)),
        pl.BlockSpec((count, HEAD_SIZE), lambda i: (0, i)),
        pl.BlockSpec((count, HEAD_SIZE), lambda i: (0, KEY_VALUE_HEADS + i)),
        pl.BlockSpec((count, 1), lambda i: (0, 0)),
        pl.BlockSpec((1, count), lambda i: (0, 0)),
        pl.BlockSpec((1, count), lambda i: (0, 0)),
    ]


def attend(queries, near, far, place_query, place_own, place_far):
    count = queries.shape[0]
    group_width = QUERY_HEADS // KEY_VALUE_HEADS

    def body(q_ref, ko_ref, vo_ref, kf_ref, vf_ref, pq_ref, po_ref, pf_ref, out_ref):
        allowed = [po_ref[...] <= pq_ref[...], pf_ref[...] <= pq_ref[...]]
        keys = [ko_ref[...], kf_ref[...]]
        for g in range(group_width):
            own, other = pair_probs(q_ref[:, head_slice(g)], keys, allowed)
            mixed = matmul(rounded(own), vo_ref[...]) + matmul(rounded(other), vf_ref[...])
            out_ref[:, head_slice(g)] = rounded(mixed)

    return pl.pallas_call(
        body,
        grid=(KEY_VALUE_HEADS,),
        in_specs=attention_specs(count),
        out_specs=pl.BlockSpec((count, group_width * HEAD_SIZE), lambda i: (0, i)),
        out_shape=jax.ShapeDtypeStruct((count, QW), jnp.bfloat16),
    )(queries, near, near, far, far, place_query, place_own, place_far)


def attend_back(queries, near, far, place_query, place_own, place_far, mixed, d_mixed):
    count = queries.shape[0]
    group_width = QUERY_HEADS // KEY_VALUE_HEADS
    heads = group_width * HEAD_SIZE

    def body(
        q_ref, ko_ref, vo_ref, kf_ref, vf_ref, pq_ref, po_ref, pf_ref, m_ref, d_ref,
        dq_ref, own_ref, far_ref,
    ):
        allowed = [po_ref[...] <= pq_ref[...], pf_ref[...] <= pq_ref[...]]
        keys = [ko_ref[...], kf_ref[...]]
        values = [vo_ref[...], vf_ref[...]]
        d_keys = [None, None]
        d_values = [None, None]
        for g in range(group_width):
            query = q_ref[:, head_slice(g)]
            upstream = d_ref[:, head_slice(g)]
            probs = pair_probs(query, keys, allowed)
            delta = jnp.sum(
                widened(upstream) * widened(m_ref[:, head_slice(g)]), axis=-1, keepdims=True
            )
            d_query = None
            for side in range(2):
                d_probs = product_transposed(upstream, values[side])
                d_scores = rounded(probs[side] * (d_probs - delta) * HEAD_SIZE ** (-0.5))
                part = matmul(d_scores, keys[side])
                d_query = part if side == 0 else d_query + part
                key_part = matmul_at(d_scores, query)
                value_part = matmul_at(rounded(probs[side]), upstream)
                d_keys[side] = key_part if g == 0 else d_keys[side] + key_part
                d_values[side] = value_part if g == 0 else d_values[side] + value_part
            dq_ref[:, head_slice(g)] = d_query
        own_ref[0] = d_keys[0]
        own_ref[1] = d_values[0]
        far_ref[0] = rounded(d_keys[1])
        far_ref[1] = rounded(d_values[1])

    return pl.pallas_call(
        body,
        grid=(KEY_VALUE_HEADS,),
        in_specs=attention_specs(count)
        + [
            pl.BlockSpec((count, heads), lambda i: (0, i)),
            pl.BlockSpec((count, heads), lambda i: (0, i)),
        ],
        out_specs=[
            pl.BlockSpec((count, heads), lambda i: (0, i)),
            pl.BlockSpec((2, count, HEAD_SIZE), lambda i: (0, 0, i)),
            pl.BlockSpec((2, count, HEAD_SIZE), lambda i: (0, 0, i)),
        ],
        out_shape=[
            jax.ShapeDtypeStruct((count, QW), jnp.float32),
            jax.ShapeDtypeStruct((2, count, KW), jnp.float32),
            jax.ShapeDtypeStruct((2, count, KW), jnp.bfloat16),
        ],
    )(
        queries, near, near, far, far, place_query, place_own, place_far, mixed, d_mixed
    )


def project_back(d_query, d_own, d_far, query_lin, key_lin, mixed, cosine, sine, query_gain, key_gain):
    count = query_lin.shape[0]

    def body(
        dq_ref, own_ref, far_ref, ql_ref, kl_ref, m_ref, c_ref, s_ref, qg_ref, kg_ref, out_ref, g_ref
    ):
        for kind, heads, base in ((0, QUERY_HEADS, 0), (1, KEY_VALUE_HEADS, QUERY_HEADS)):
            gain = (qg_ref, kg_ref)[kind][...]
            gathered = None
            for h in range(heads):
                if kind == 0:
                    upstream = dq_ref[:, head_slice(h)]
                else:
                    upstream = own_ref[0, :, head_slice(h)] + widened(far_ref[0, :, head_slice(h)])
                part = (ql_ref, kl_ref)[kind][:, head_slice(h)]
                scale = rms_scale(part)
                unit = part * scale
                d_unit = upstream * c_ref[...] - swapped(upstream) * s_ref[...]
                share = jnp.sum(d_unit * unit, axis=0, keepdims=True)
                gathered = share if h == 0 else gathered + share
                out_ref[:, head_slice(base + h)] = rounded(norm_back(d_unit, unit, scale, gain))
            g_ref[kind : kind + 1, :] = gathered
        out_ref[:, QW + KW : QW + 2 * KW] = rounded(own_ref[1] + widened(far_ref[1]))
        out_ref[:, QW + 2 * KW :] = m_ref[...]

    return pl.pallas_call(
        body,
        out_shape=[
            jax.ShapeDtypeStruct((count, 2 * QW + 2 * KW), jnp.bfloat16),
            jax.ShapeDtypeStruct((2, HEAD_SIZE), jnp.float32),
        ],
    )(d_query, d_own, d_far, query_lin, key_lin, mixed, cosine, sine, query_gain[None], key_gain[None])


def attention_weight_grads(d_rows, normed, d_residual):
    low = rounded(matmul_at(d_rows[:, : QW + 2 * KW], normed))
    return jnp.concatenate([low, rounded(matmul_at(d_rows[:, QW + 2 * KW :], d_residual))])


def attention_block_grads(d_rows, normed, d_residual, plan, block, halves):
    count, width = normed.shape
    split = QW + 2 * KW
    half = block // halves

    def body(plan_ref, d_ref, n_ref, r_ref, kept_ref, sent_ref):
        owner = plan_ref[pl.program_id(0)]
        start = owner * block
        core = plan_ref[2]

        def store(grads):
            @pl.when(core == 0)
            def _():
                kept_ref[0] = rounded(grads[:half])
                sent_ref[0] = rounded(grads[half:])

            @pl.when(core == 1)
            def _():
                kept_ref[0] = rounded(grads[half:])
                sent_ref[0] = rounded(grads[:half])

        @pl.when(start + block <= split)
        def _():
            store(matmul_at(d_ref[...], n_ref[...]))

        @pl.when(start >= split)
        def _():
            store(matmul_at(d_ref[...], r_ref[...]))

        @pl.when((start < split) & (start + block > split))
        def _():
            rows = d_ref[...]
            place = start + lax.broadcasted_iota(jnp.int32, rows.shape, 1)
            zero = jnp.zeros_like(rows)
            store(
                matmul_at(jnp.where(place < split, rows, zero), n_ref[...])
                + matmul_at(jnp.where(place < split, zero, rows), r_ref[...])
            )

    return pl.pallas_call(
        body,
        grid_spec=pltpu.PrefetchScalarGridSpec(
            num_scalar_prefetch=1,
            grid=(2,),
            in_specs=[
                pl.BlockSpec((count, block), lambda i, plan: (0, plan[i])),
                pl.BlockSpec((count, width), lambda i, plan: (0, 0)),
                pl.BlockSpec((count, width), lambda i, plan: (0, 0)),
            ],
            out_specs=[
                pl.BlockSpec((1, half, width), lambda i, plan: (i, 0, 0)),
                pl.BlockSpec((1, half, width), lambda i, plan: (i, 0, 0)),
            ],
        ),
        out_shape=[jax.ShapeDtypeStruct((2, half, width), jnp.bfloat16)] * 2,
    )(plan, d_rows, normed, d_residual)


def swiglu_block_grads(d_gate, d_upper, hidden_b, normed, cotan, number, units, halves):
    count, width = normed.shape
    half = units // halves
    if units % HEAD_SIZE:
        cols = slice(number * units, (number + 1) * units)
        d_gate, d_upper, hidden_b, number = d_gate[:, cols], d_upper[:, cols], hidden_b[:, cols], 0

    def body(g_ref, u_ref, h_ref, n_ref, c_ref, *out_refs):
        step = pl.program_id(0)
        for kind, left, right in ((0, g_ref, n_ref), (1, u_ref, n_ref), (2, h_ref, c_ref)):

            @pl.when(step == kind)
            def _():
                grads = matmul_at(left[...], right[...])
                for index, out_ref in enumerate(out_refs):
                    out_ref[0] = rounded(grads[index * half : (index + 1) * half])

    return pl.pallas_call(
        body,
        grid=(3,),
        in_specs=[pl.BlockSpec((count, units), lambda i: (0, number))] * 3
        + [pl.BlockSpec((count, width), lambda i: (0, 0))] * 2,
        out_specs=[pl.BlockSpec((1, half, width), lambda i: (i, 0, 0))] * halves,
        out_shape=[jax.ShapeDtypeStruct((3, half, width), jnp.bfloat16)] * halves,
    )(d_gate, d_upper, hidden_b, normed, cotan)


def build(mesh):
    rep_size = mesh.shape["rep"]
    grp_size = mesh.shape["grp"]
    pair = 2 if rep_size % 2 == 0 else 1
    lanes = rep_size // pair
    plus_steps = grp_size // 2
    minus_steps = grp_size - 1 - plus_steps

    def core_swap(values):
        return lax.ppermute(values, "rep", [(i, i ^ 1) for i in range(rep_size)])

    def lane_swap(values, offset):
        return lax.ppermute(values, "rep", [(i, i ^ (offset * pair)) for i in range(rep_size)])

    def ctx_swap(values):
        return lax.ppermute(values, "ctx", [(0, 1), (1, 0)])

    def grp_shift(values, offset):
        return lax.ppermute(values, "grp", [(i, (i + offset) % grp_size) for i in range(grp_size)])

    def grp_gather(block):
        blocks = {0: block}
        for step in range(1, plus_steps + 1):
            blocks[step] = grp_shift(blocks[step - 1], 1)
        for step in range(1, minus_steps + 1):
            blocks[grp_size - step] = grp_shift(blocks[(grp_size - step + 1) % grp_size], -1)
        return blocks

    def grp_gather_in_turn(block, after):
        blocks = {0: block}
        for step in range(1, plus_steps + 1):
            after = grp_shift(tie(blocks[step - 1], after), 1)
            blocks[step] = after
            if step <= minus_steps:
                k = grp_size - step
                after = grp_shift(tie(blocks[(k + 1) % grp_size], after), -1)
                blocks[k] = after
        return blocks

    reduce_order = (
        list(range(plus_steps, 0, -1))
        + list(range(plus_steps + 1, grp_size))
        + [0]
    )

    class GrpReduce:
        def __init__(self):
            self.low = None
            self.high = None

        def push(self, k, block):
            if k == 0:
                total = widened(block)
                for part in (self.low, self.high):
                    if part is not None:
                        total = total + widened(part)
                return total
            if k <= plus_steps:
                if self.low is not None:
                    block = added(block, self.low)
                self.sent = block
                self.low = grp_shift(block, -1)
            else:
                if self.high is not None:
                    block = added(block, self.high)
                self.sent = block
                self.high = grp_shift(block, 1)
            return None

    def sum_steps():
        steps = [lambda v: core_swap(v)] if pair == 2 else []
        steps.append(lambda v: ctx_swap(v))
        for bit in range((grp_size - 1).bit_length()):
            steps.append(
                lambda v, bit=bit: lax.ppermute(
                    v, "grp", [(i, i ^ (1 << bit)) for i in range(grp_size)]
                )
            )
        for bit in range((lanes - 1).bit_length()):
            steps.append(lambda v, bit=bit: lane_swap(v, 1 << bit))
        return steps

    def shards(
        hidden,
        positions,
        cotangent,
        attention_params,
        attention_moment,
        attention_variance,
        swiglu_params,
        swiglu_moment,
        swiglu_variance,
        norm_gains,
        gains_moment,
        gains_variance,
    ):
        sequence_count, token_count, model_width = hidden.shape
        row_number = sequence_count * token_count
        rep_at = lax.axis_index("rep")
        grp_at = lax.axis_index("grp")
        ctx_at = lax.axis_index("ctx")
        core_at = rep_at % pair

        gain_rows = norm_gains.shape[0]
        gains_pair = rounded(norm_gains)[None]
        gains_other = ctx_swap(gains_pair)
        both = jnp.where(
            ctx_at == 0,
            jnp.concatenate([gains_pair, gains_other]),
            jnp.concatenate([gains_other, gains_pair]),
        )
        gains_all = jnp.zeros((grp_size, 2, gain_rows), jnp.bfloat16)
        for k in range(grp_size):
            arrived = both if k == 0 else grp_shift(both, k)
            gains_all = lax.dynamic_update_slice(
                gains_all, arrived[None], ((grp_at - k) % grp_size, 0, 0)
            )
        gains_f = widened(gains_all.reshape(-1))
        first_gain = gains_f[:model_width]
        second_gain = gains_f[model_width : 2 * model_width]
        query_gain = gains_f[2 * model_width : 2 * model_width + HEAD_SIZE]
        key_gain = gains_f[2 * model_width + HEAD_SIZE :]

        att_rows = attention_params.shape[0]
        half_rows = att_rows // pair
        lane_rows = half_rows // lanes
        lane_at = rep_at // pair
        attention_own = rounded(attention_params)
        half_own = lax.dynamic_slice_in_dim(attention_own, core_at * half_rows, half_rows, 0)
        mine_own = lax.dynamic_slice_in_dim(attention_own, core_at * half_rows + lane_at * lane_rows, lane_rows, 0)
        near = grp_gather(mine_own)
        last_near = near[plus_steps]
        pieces = [(ctx_swap(half_own), 0, 1, 0)]
        last_far = None
        for k in [1] + list(range(plus_steps + 1, grp_size)) + list(range(2, plus_steps + 1)):
            mine = near[k]
            others = [lane_swap(mine, lane) for lane in range(1, lanes)]
            far = ctx_swap(mine)
            if k == 1:
                far_others = [ctx_swap(other) for other in others]
            else:
                far_others = [lane_swap(far, lane) for lane in range(1, lanes)]
            last_far = far
            for plane, group in ((0, [mine] + others), (1, [far] + far_others)):
                pieces += [(block, k, plane, lane) for lane, block in enumerate(group)]
        units = swiglu_params.shape[0]
        piece = units // rep_size
        swiglu_t = jnp.transpose(swiglu_params, (1, 0, 2))

        def own_piece(offset, at):
            return rounded(lax.dynamic_slice_in_dim(swiglu_t, (at ^ offset) * piece, piece, 1))

        ring = grp_gather_in_turn(own_piece(0, rep_at), last_near)
        where = jnp.stack([grp_at, ctx_at, core_at, lane_at]).astype(jnp.int32)
        att_shape = (grp_size, 2, pair, lanes, lane_rows, model_width)

        def spot(k, plane, core, lane):
            def index(ref):
                start = ((ref[0] + (grp_size - k)) % grp_size, ref[1] ^ plane, ref[2] ^ core)
                return start if lane is None else start + (ref[3] ^ lane,)

            return index

        copies = [
            (
                attention_own.reshape(pair, lanes, lane_rows, model_width),
                0,
                lambda ref: (ref[0], ref[1]),
                None,
            )
        ]
        for block, k, plane, lane in pieces:
            shape = (lane_rows, model_width)
            if block.shape[0] != lane_rows:
                shape, lane = (lanes,) + shape, None
            copies.append((block.reshape(shape), 0, spot(k, plane, 0, lane), None))
            if pair == 2:
                other = core_swap(block).reshape(shape)
                copies.append((other, 0, spot(k, plane, 1, lane), None))
        early = 3 + 2 * pair * lanes * (plus_steps + minus_steps) // 2
        late = copies[early:]
        late[-1] = (tie(late[-1][0], ring[1]),) + late[-1][1:]
        attention_all = copied_into(None, [att_shape], where, copies[:early])
        attention_all = copied_into(attention_all, [att_shape], where, late)[0]
        attention_all = attention_all.reshape(-1, model_width)

        cotan_rows = cotangent.reshape(row_number, model_width)
        cotan_both = jnp.concatenate([cotan_rows, ctx_swap(tie(cotan_rows, last_far))])

        late_at = tie(rep_at, ring[1])
        weight_shapes = [(grp_size * units, model_width)] * 3

        def put(values, k, core, lane):
            start = k * units + (core * lanes + lane) * piece
            return [(values, j, lambda ref: (pl.ds(start, piece),), j) for j in range(3)]

        weight_copies = {}
        for k in range(grp_size):
            weight_copies[k] = []
            for lane in range(lanes):
                if k == 0:
                    for core in range(pair):
                        own = own_piece(lane * pair + core, late_at)
                        weight_copies[k] += put(own, k, core, lane)
                    continue
                arrived = ring[k] if lane == 0 else lane_swap(ring[k], lane)
                weight_copies[k] += put(arrived, k, 0, lane)
                if pair == 2:
                    weight_copies[k] += put(core_swap(arrived), k, 1, lane)
        weights = copied_into(
            None,
            weight_shapes,
            where,
            [c for k in range(grp_size) if k != plus_steps for c in weight_copies[k]],
        )
        weights = copied_into(weights, weight_shapes, where, weight_copies[plus_steps])
        w_gate, w_up, w_down = weights

        w_output = attention_all[QW + 2 * KW :]
        w_qkv = attention_all[: QW + 2 * KW]
        start_row = ctx_at * token_count
        places_own = lax.dynamic_slice_in_dim(positions, start_row, token_count, 1)
        places_far = lax.dynamic_slice_in_dim(
            positions, (1 - ctx_at) * token_count, token_count, 1
        )
        place_query = places_own.reshape(row_number, 1)
        inputs = widened(hidden.reshape(row_number, model_width))
        scale_one = rms_scale(inputs)
        unit_one = inputs * scale_one
        first_normed = rounded(unit_one * first_gain)
        cosine_table, sine_table = rotate_tables(places_own.reshape(-1))
        blocks = 2 * HEAD_SIZE
        gain_table = jnp.stack(
            [query_gain] * (QW // blocks)
            + [key_gain] * (KW // blocks)
            + [jnp.ones_like(key_gain)] * (KW // blocks)
        )[:, None]
        tables = (cosine_table, sine_table, gain_table)
        key_lin, key_value = project(
            first_normed, attention_all, *tables, QW, QW + 2 * KW
        )
        key_value_far = ctx_swap(key_value)
        query_lin, queries = project(first_normed, attention_all, *tables, 0, QW)
        mixed_rows = attend(queries, key_value, key_value_far, place_query, places_own, places_far)
        residual = inputs + matmul(mixed_rows, w_output)
        scale_two = rms_scale(residual)
        unit_two = residual * scale_two
        normed_two = rounded(unit_two * second_gain)
        normed_both = jnp.concatenate([normed_two, ctx_swap(normed_two)])

        gate_values, up_values, sigmoid_gate, active, hidden_b = gate_forward(
            normed_both, w_gate, w_up
        )
        d_hidden = product_transposed(cotan_both, w_down)
        d_gate, d_upper = gate_backward(d_hidden, gate_values, up_values, sigmoid_gate, active)
        d_normed_both = matmul(d_gate, w_gate) + matmul(d_upper, w_up)
        d_normed_sent = rounded(d_normed_both[row_number:])
        d_normed_back = ctx_swap(d_normed_sent)
        kept_blocks, lane_sent, lane_back = [], [], []

        def start_swiglu(number, *after):
            k = reduce_order[number]
            operands = lax.optimization_barrier((d_gate, d_upper, hidden_b, *after))[:3]
            parts = swiglu_block_grads(*operands, normed_both, cotan_both, k, units, pair)
            mark = parts[0]
            if pair == 2:
                parts = [parts[0], core_swap(parts[1])]

            def lane_block(lane):
                rows = slice(lane * piece, (lane + 1) * piece)
                return sum(widened(part[:, rows]) for part in parts)

            kept_blocks.append(lane_block(0))
            lane_sent.append([rounded(lane_block(lane)) for lane in range(1, lanes)])
            lane_back.append([lane_swap(b, i + 1) for i, b in enumerate(lane_sent[-1])])
            return mark

        early_blocks = grp_size // 2
        mark = d_normed_sent
        for number in range(early_blocks):
            mark = start_swiglu(number, mark)
        d_normed_two = d_normed_both[:row_number] + widened(tie(d_normed_back, mark))

        reducer = GrpReduce()

        def reduce_swiglu(number):
            total = kept_blocks[number]
            for block in lane_back[number]:
                total = total + widened(block)
            return reducer.push(reduce_order[number], rounded(total))

        def spread(values, axis):
            blocks = {}
            for lane in range(lanes):
                blocks[lane * pair] = values if lane == 0 else lane_swap(values, lane)
                if pair == 2:
                    blocks[lane * pair + 1] = core_swap(blocks[lane * pair])
            count = values.shape[axis]
            shape = list(values.shape)
            shape[axis] = count * rep_size
            result = jnp.zeros(shape, values.dtype)
            for offset, block in blocks.items():
                result = lax.dynamic_update_slice_in_dim(
                    result, block, (rep_at ^ offset) * count, axis
                )
            return result

        grad_second = jnp.sum(d_normed_two * unit_two, axis=0)
        d_residual = widened(cotan_rows) + norm_back(d_normed_two, unit_two, scale_two, second_gain)
        d_residual_b = rounded(d_residual)
        mixed_gradient_local = rounded(product_transposed(d_residual_b, w_output))
        mixed_gradient_local = tie(mixed_gradient_local, *lane_sent[early_blocks - 1])
        d_query, d_own, d_far = attend_back(
            queries,
            key_value,
            key_value_far,
            place_query,
            places_own,
            places_far,
            mixed_rows,
            mixed_gradient_local,
        )
        d_back = ctx_swap(d_far)
        for number in range(early_blocks, grp_size - 1):
            mark = start_swiglu(number, d_far)
        reduce_swiglu(0)
        d_back = tie(d_back, reducer.sent, mark)
        d_rows, head_gains = project_back(
            d_query,
            d_own,
            d_back,
            query_lin,
            key_lin,
            mixed_rows,
            cosine_table,
            sine_table,
            query_gain,
            key_gain,
        )
        by_block = att_rows % HEAD_SIZE == 0
        if not by_block:
            attention_full = attention_weight_grads(d_rows, first_normed, d_residual_b).reshape(
                grp_size, 2, pair, half_rows, model_width
            )

        def block_of(k, plane, core):
            return lax.dynamic_slice(
                attention_full,
                ((grp_at - k) % grp_size, ctx_at ^ plane, core_at ^ core, 0, 0),
                (1, 1, 1, half_rows, model_width),
            ).reshape(half_rows, model_width)

        def halves_of(k):
            if by_block and pair == 2:
                owner = (grp_at - k) % grp_size * 2
                plan = jnp.stack([owner + (1 - ctx_at), owner + ctx_at, core_at]).astype(jnp.int32)
                return attention_block_grads(
                    d_rows, first_normed, d_residual_b, plan, att_rows, pair
                )
            return [
                jnp.stack([block_of(k, plane, core) for plane in (1, 0)]) for core in range(pair)
            ]

        att_reducer = GrpReduce()
        parts_of = {}
        for number, k in enumerate(reduce_order):
            parts = halves_of(k)
            if number == 0:
                mark = parts[0]
            if pair == 2:
                parts = [parts[0], core_swap(parts[1])]
            parts_of[k] = parts
        start_swiglu(grp_size - 1, mark)
        layer_both = matmul(tie(hidden_b, mark), w_down)
        layer_back = ctx_swap(rounded(layer_both[row_number:]))
        d_normed_one = matmul(tie(d_rows, mark)[:, : QW + 2 * KW], w_qkv)
        grad_first = jnp.sum(d_normed_one * unit_one, axis=0)
        gains_total = jnp.concatenate([grad_first, grad_second, head_gains.reshape(-1)])
        gain_steps = sum_steps()
        attention_half = None
        for number, k in enumerate(reduce_order):
            far = rounded(sum(widened(part[0]) for part in parts_of[k]))
            far_back = ctx_swap(far)
            if number and gain_steps:
                gains_total = gains_total + gain_steps.pop(0)(gains_total)
                far_back = tie(far_back, gains_total)
            if number < len(reduce_order) - 2:
                reduce_swiglu(number + 1)
                far_back = tie(far_back, reducer.sent)
            total = sum(widened(part[1]) for part in parts_of[k]) + widened(far_back)
            attention_half = att_reducer.push(k, rounded(total))
        for step in gain_steps:
            gains_total = gains_total + step(gains_total)
        layer_sum = (residual + layer_both[:row_number]) + widened(layer_back)
        layer_output = rounded(layer_sum).reshape(sequence_count, token_count, model_width)
        swiglu_piece = rounded(reduce_swiglu(len(reduce_order) - 1))
        swiglu_grad = jnp.transpose(widened(spread(swiglu_piece, 1)), (1, 0, 2))
        attention_half = tie(rounded(attention_half), swiglu_piece)
        bit = 1
        while bit < lanes:
            attention_half = added(attention_half, lane_swap(attention_half, bit))
            bit *= 2
        attention_grad = attention_half
        if pair == 2:
            attention_grad = jnp.zeros((att_rows, model_width), jnp.bfloat16)
            for core, block in ((0, attention_half), (1, core_swap(attention_half))):
                attention_grad = lax.dynamic_update_slice(
                    attention_grad, block, ((core_at ^ core) * half_rows, 0)
                )
        attention_grad = widened(attention_grad)

        hidden_grad = d_residual + norm_back(d_normed_one, unit_one, scale_one, first_gain)
        gains_grad = lax.dynamic_slice_in_dim(
            gains_total, (grp_at * 2 + ctx_at) * gain_rows, gain_rows, 0
        )
        attention_new = adam_update(
            attention_params, attention_moment, attention_variance, attention_grad, DECAY
        )
        swiglu_new = adam_update(swiglu_params, swiglu_moment, swiglu_variance, swiglu_grad, DECAY)
        gains_new = adam_update(norm_gains, gains_moment, gains_variance, gains_grad, 0.0)
        return (
            layer_output,
            hidden_grad.reshape(sequence_count, token_count, model_width),
            attention_grad,
            swiglu_grad,
            gains_grad,
            attention_new[0],
            attention_new[1],
            attention_new[2],
            swiglu_new[0],
            swiglu_new[1],
            swiglu_new[2],
            gains_new[0],
            gains_new[1],
            gains_new[2],
        )

    return shards


def solution(mesh):
    in_specs = (
        P(("rep", "grp"), "ctx", None),
        P(("rep", "grp"), None),
        P(("rep", "grp"), "ctx", None),
        P(("grp", "ctx"), None),
        P(("grp", "ctx"), None),
        P(("grp", "ctx"), None),
        P(("grp", "ctx"), None, None),
        P(("grp", "ctx"), None, None),
        P(("grp", "ctx"), None, None),
        P(("grp", "ctx")),
        P(("grp", "ctx")),
        P(("grp", "ctx")),
    )
    out_specs = (
        P(("rep", "grp"), "ctx", None),
        P(("rep", "grp"), "ctx", None),
        P(("grp", "ctx"), None),
        P(("grp", "ctx"), None, None),
        P(("grp", "ctx")),
        P(("grp", "ctx"), None),
        P(("grp", "ctx"), None),
        P(("grp", "ctx"), None),
        P(("grp", "ctx"), None, None),
        P(("grp", "ctx"), None, None),
        P(("grp", "ctx"), None, None),
        P(("grp", "ctx")),
        P(("grp", "ctx")),
        P(("grp", "ctx")),
    )
    body = build(mesh)

    return jax.shard_map(body, mesh=mesh, in_specs=in_specs, out_specs=out_specs, check_vma=False)
```
